32 devices in a mesh: dp: 4 (over y, x), ctx: 8 (over z, core).
Axes of the slice: x: 2, y: 2, z: 4, core: 2. Of those that a mesh axis runs over, the one named last changes fastest.
Arguments:
- inputs: bfloat16 [4, 2048, 4096], P('dp', 'ctx'), may hold values from -6 to 6
- query_weight: bfloat16 [4096, 128], P('dp'), may hold values from -0.09375 to 0.09375
- key_weight: bfloat16 [4096, 128], P('dp'), may hold values from -0.09375 to 0.09375
- value_weight: bfloat16 [4096, 2048], P('dp'), may hold values from -0.09375 to 0.09375
- lambda_weight: bfloat16 [4096, 320], P('dp'), may hold values from -0.09375 to 0.09375
- log_decay: float32 [4, 2048, 16], P('dp', 'ctx'), may hold values from -1 to 0, as said below
- norm_gain: float32 [2048], replicated, may hold values from 0.5 to 1.5
Outputs:
- outputs: bfloat16 [4, 2048, 2048], P('dp', 'ctx')
The draws below stay inside these ranges and needn't reach their ends.
Inputs may be any that keep to these rules, and one draw needn't show every extreme that they name: `log_decay`: entries are not positive.
All inputs are finite; a program needn't handle non-finite values.
Results may differ from the reference program's by a relative error of at most 0.0072.
Values may be sent and summed in bfloat16 or wider, within the bound.
A program may use at most 128 MiB of HBM per device.

```python
import math
import jax
import jax.numpy as jnp
from jax import lax

D = 4096
HEADS = 16
HEAD = 128
STATE = 128
LAMBDAS = 20
TOK_DEV = 256
SEQUENCE_TOTAL = 4
SEQUENCE_SPAN = 2048
N_CTX = 8


def draw_log_decay(key, part):
    key_kind = jax.random.fold_in(key, 11)
    key_slow = jax.random.fold_in(key, 12)
    key_pick = jax.random.fold_in(key, 13)
    key_token = jax.random.fold_in(key, 14)
    key_block = jax.random.fold_in(key, 15)
    key_spurt = jax.random.fold_in(key, 16)
    key_keep = jax.random.fold_in(key, 17)
    key_width = jax.random.fold_in(key, 18)
    key_offset = jax.random.fold_in(key, 19)
    key_mass = jax.random.fold_in(key, 20)
    block_count = SEQUENCE_SPAN // TOK_DEV
    mixed_count = max(HEADS // 2, 1)
    fast_share = 0.5
    order = jax.random.permutation(key_kind, HEADS)
    mixed_head = order < mixed_count
    slow_rate = jnp.exp(jax.random.uniform(key_slow, (HEADS,), jnp.float32, math.log(0.05), math.log(0.4))) / SEQUENCE_SPAN
    block_shape = (SEQUENCE_TOTAL, block_count, 1, HEADS)
    fast_block = jnp.logical_and(jax.random.uniform(key_pick, block_shape, jnp.float32) < fast_share, mixed_head[None, None, None, :])
    token = jax.random.uniform(key_token, (SEQUENCE_TOTAL, block_count, TOK_DEV, HEADS), jnp.float32, 0.5, 2.0)
    blocks = jnp.exp(jax.random.uniform(key_block, block_shape, jnp.float32, -0.7, 0.7))
    slow_part = token * blocks * slow_rate[None, None, None, :]
    width = jax.random.randint(key_width, block_shape, max(TOK_DEV // 8, 1), TOK_DEV + 1)
    offset = jax.random.randint(key_offset, block_shape, 0, TOK_DEV) % (TOK_DEV - width + 1)
    position_in = jnp.arange(TOK_DEV, dtype=jnp.int32)[None, None, :, None]
    inside = jnp.logical_and(position_in >= offset, position_in < offset + width)
    mass = jnp.exp(jax.random.uniform(key_mass, block_shape, jnp.float32, math.log(8.0), math.log(16.0)))
    fast_part = jnp.where(inside, jnp.minimum(mass / width.astype(jnp.float32) * token, 1.0), slow_part)
    elementwise_rate = jnp.where(fast_block, fast_part, slow_part).reshape(SEQUENCE_TOTAL, SEQUENCE_SPAN, HEADS)
    spurt_index = jax.random.randint(key_spurt, (SEQUENCE_TOTAL, 3), 0, SEQUENCE_SPAN)
    token_place = jnp.arange(SEQUENCE_SPAN, dtype=jnp.int32)
    spurt_mask = jnp.any(token_place[None, :, None] == spurt_index[:, None, :], axis=-1)
    kept_entries = jax.random.uniform(key_keep, (SEQUENCE_TOTAL, SEQUENCE_SPAN, 1), jnp.float32, 0.55, 0.8)
    spurt_portion = jnp.where(spurt_mask[:, :, None], jnp.log(kept_entries), 0.0)
    return jnp.maximum(spurt_portion - elementwise_rate, -1.0).astype(jnp.float32)


def level_of(stream_key, extent, cuts, low, high):
    factor_of = 1.0
    for axis_at, shards_of in cuts:
        steps = jax.random.uniform(jax.random.fold_in(jax.random.fold_in(stream_key, 6), axis_at), (shards_of,), jnp.float32, low / len(cuts), high / len(cuts))
        factor_of = factor_of * jnp.repeat(jnp.exp(steps), extent[axis_at] // shards_of).reshape((-1,) + (1,) * (len(extent) - 1 - axis_at))
    return factor_of


def scatter_about(stream_key, shape, deviation, most, shards=(), held_as=jnp.bfloat16):
    drawn = jax.random.normal(stream_key, shape, jnp.float32) * deviation
    if len(shards) > 0:
        drawn = level_of(stream_key, shape, shards, -0.22, 0.18) * drawn
    return jnp.clip(drawn, min=-most, max=most).astype(held_as)


def setup_inputs(seed: int = 0) -> dict:
    keys = jax.random.split(jax.random.key(seed), 8)
    return {
        "inputs": scatter_about(keys[0], (SEQUENCE_TOTAL, SEQUENCE_SPAN, D), 1.0, 6.0, ((0, 4), (1, 8))),
        "query_weight": scatter_about(keys[1], (D, STATE), D ** -0.5, 0.09375, ((0, 4),)),
        "key_weight": scatter_about(keys[2], (D, STATE), D ** -0.5, 0.09375, ((0, 4),)),
        "value_weight": scatter_about(keys[3], (D, HEADS * HEAD), D ** -0.5, 0.09375, ((0, 4),)),
        "lambda_weight": scatter_about(keys[4], (D, HEADS * LAMBDAS), D ** -0.5, 0.09375, ((0, 4),)),
        "log_decay": draw_log_decay(jax.random.fold_in(keys[7], 71), 0),
        "norm_gain": jnp.clip(1.0 + 0.1 * jax.random.normal(keys[6], (HEADS * HEAD,), jnp.float32), 0.5, 1.5),
    }


HIGHEST = lax.Precision.HIGHEST

def level_masks(length):
    depth = length.bit_length() - 1
    token_place = jnp.arange(length, dtype=jnp.int32)
    differ = jnp.bitwise_xor(token_place[:, None], token_place[None, :])
    level = jnp.zeros((length, length), jnp.int32)
    for power in range(depth):
        level = level + (differ >= 1 << power).astype(jnp.int32)
    levels = jnp.arange(depth + 1, dtype=jnp.int32)
    return (level[None, :, :] == levels[:, None, None]).astype(jnp.float32)

def block_terms(query_rows, key_rows, value_rows, lambdas, log_decay, masks):
    length, heads = log_decay.shape
    state_dim = query_rows.shape[1]
    head_dim = value_rows.shape[1] // heads
    inner = masks.shape[0]
    weights_all = lambdas.reshape(length, heads, -1)
    cumulative = jnp.cumsum(log_decay, axis=0)
    scores = jnp.dot(query_rows, key_rows.T, preferred_element_type=jnp.float32) / math.sqrt(state_dim)
    level_weight = jnp.einsum('lts,thl->hts', masks, weights_all[:, :, :inner], precision=HIGHEST)
    token_place = jnp.arange(length, dtype=jnp.int32)
    causal = token_place[:, None] >= token_place[None, :]
    spread = jnp.transpose(cumulative)
    distance = spread[:, :, None] - spread[:, None, :]
    decay = jnp.exp(jnp.where(causal[None], distance, -jnp.inf))
    mix = (level_weight * decay * scores[None]).astype(jnp.bfloat16)
    values = value_rows.reshape(length, heads, head_dim)
    near = jnp.einsum('hts,shd->thd', mix.astype(jnp.float32), values.astype(jnp.float32), precision=HIGHEST)
    remain = jnp.exp(cumulative[-1][None, :] - cumulative)
    keyed = (key_rows.astype(jnp.float32)[:, None, :] * remain[:, :, None]).astype(jnp.bfloat16)
    state = jnp.einsum('chs,chd->hsd', keyed.astype(jnp.float32), values.astype(jnp.float32), precision=HIGHEST)
    total = jnp.exp(cumulative[-1])
    return (near, state, total, cumulative, weights_all)

def finish(mixed, norm_gain):
    heads = mixed.shape[-2]
    mean_square = lax.optimization_barrier(jnp.mean(mixed * mixed, axis=-1, keepdims=True))
    return (mixed * lax.rsqrt(mean_square + 1e-05) * norm_gain.reshape(heads, -1)).astype(jnp.bfloat16)

def reference(inputs, query_weight, key_weight, value_weight, lambda_weight, log_decay, norm_gain):
    bits = N_CTX.bit_length() - 1
    masks = level_masks(TOK_DEV)
    inner = masks.shape[0]
    scale = 1.0 / math.sqrt(STATE)

    def one_sequence(pair):
        sequence, decays = pair
        query_rows = jnp.dot(sequence, query_weight, preferred_element_type=jnp.float32).astype(jnp.bfloat16)
        key_rows = jnp.dot(sequence, key_weight, preferred_element_type=jnp.float32).astype(jnp.bfloat16)
        value_rows = jnp.dot(sequence, value_weight, preferred_element_type=jnp.float32).astype(jnp.bfloat16)
        lambdas = jax.nn.softplus(jnp.dot(sequence, lambda_weight, preferred_element_type=jnp.float32))

        def per_block(pieces):
            return block_terms(pieces[0], pieces[1], pieces[2], pieces[3], pieces[4], masks)
        near, state, total, cumulative, weights_all = lax.map(per_block, (query_rows.reshape(N_CTX, TOK_DEV, -1), key_rows.reshape(N_CTX, TOK_DEV, -1), value_rows.reshape(N_CTX, TOK_DEV, -1), lambdas.reshape(N_CTX, TOK_DEV, -1), decays.reshape(N_CTX, TOK_DEV, -1)))
        block_index = jnp.arange(N_CTX, dtype=jnp.int32)
        block_state = state
        block_total = total
        carry_decay = jnp.ones_like(total)
        query_blocks = query_rows.reshape(N_CTX, TOK_DEV, -1).astype(jnp.float32)
        mixed = near
        for level_bit in range(bits):
            partner = jnp.bitwise_xor(block_index, jnp.int32(1 << level_bit))
            other_state = block_state[partner]
            other_total = block_total[partner]
            upper = (block_index >> level_bit & 1).astype(jnp.float32)
            carried = (carry_decay[:, :, None, None] * other_state).astype(jnp.bfloat16)
            reach = jnp.einsum('jts,jhsd->jthd', query_blocks, carried.astype(jnp.float32), precision=HIGHEST)
            factor = weights_all[:, :, :, inner + level_bit] * jnp.exp(cumulative) * (scale * upper[:, None, None])
            mixed = mixed + factor[..., None] * reach
            if level_bit + 1 < bits:
                flag = upper[:, None, None, None] > 0
                block_state = jnp.where(flag, block_total[:, :, None, None] * other_state + block_state, other_total[:, :, None, None] * block_state + other_state)
                carry_decay = jnp.where(upper[:, None] > 0, other_total * carry_decay, carry_decay)
                block_total = block_total * other_total
        return finish(mixed, norm_gain).reshape(SEQUENCE_SPAN, -1)
    return lax.map(one_sequence, (inputs, log_decay))
```

```python
import functools
import math

import jax
import jax.numpy as jnp
from jax import lax
from jax.experimental import pallas as pl
from jax.experimental.pallas import tpu as pltpu
from jax.sharding import PartitionSpec as P

HIGHEST = lax.Precision.HIGHEST
MESH = pl.DeviceIdType.MESH
VMEM_LIMIT = 63 * 1024 * 1024


def from_partner(block, axis, stride):
    count = lax.axis_size(axis)
    route = []
    for low in range(count):
        high = low | 1 << stride
        if high != low and high < count:
            route += [(low, high), (high, low)]
    return lax.ppermute(block, axis, route)


def level_masks(length):
    depth = length.bit_length() - 1
    token_place = jnp.arange(length, dtype=jnp.int32)
    differ = jnp.bitwise_xor(token_place[:, None], token_place[None, :])
    level = jnp.zeros((length, length), jnp.int32)
    for power in range(depth):
        level = level + (differ >= 1 << power).astype(jnp.int32)
    levels = jnp.arange(depth + 1, dtype=jnp.int32)
    return (level[None, :, :] == levels[:, None, None]).astype(jnp.float32)


def block_terms(query_rows, key_rows, value_rows, lambdas, log_decay, masks):
    length, heads = log_decay.shape
    state_dim = query_rows.shape[1]
    head_dim = value_rows.shape[1] // heads
    inner = masks.shape[0]
    weights_all = lambdas.reshape(length, heads, -1)
    cumulative = jnp.cumsum(log_decay, axis=0)
    scores = lax.dot_general(
        query_rows, key_rows, (((1,), (1,)), ((), ())), preferred_element_type=jnp.float32
    ) / math.sqrt(state_dim)
    level_weight = jnp.einsum("lts,thl->hts", masks, weights_all[:, :, :inner], precision=HIGHEST)
    token_place = jnp.arange(length, dtype=jnp.int32)
    causal = token_place[:, None] >= token_place[None, :]
    spread = jnp.transpose(cumulative)
    distance = spread[:, :, None] - spread[:, None, :]
    decay = jnp.exp(jnp.where(causal[None], distance, -jnp.inf))
    mix = (level_weight * decay * scores[None]).astype(jnp.bfloat16)
    values = value_rows.reshape(length, heads, head_dim)
    near = jnp.einsum("hts,shd->thd", mix, values, preferred_element_type=jnp.float32)
    remain = jnp.exp(cumulative[-1][None, :] - cumulative)
    keyed = (key_rows.astype(jnp.float32)[:, None, :] * remain[:, :, None]).astype(jnp.bfloat16)
    state = jnp.einsum("chs,chd->hsd", keyed, values, preferred_element_type=jnp.float32)
    total = jnp.exp(cumulative[-1])
    return (near, state, total, cumulative, weights_all)


def finish(mixed, norm_gain):
    heads = mixed.shape[-2]
    mean_square = jnp.mean(mixed * mixed, axis=-1, keepdims=True)
    return (mixed * lax.rsqrt(mean_square + 1e-05) * norm_gain.reshape(heads, -1)).astype(
        jnp.bfloat16
    )


CHUNKS = 8
SHARED = 2


def gather_kernel(x_ref, a_ref, v_ref, qk_ref, lam_ref, val_ref, big_a, big_v, acc_a, acc_v,
                  direct_sem, core_sem, send_sem, relay_sem, z_sem, fwd_sem):
    depth = a_ref.shape[0]
    rows = depth // CHUNKS
    half = rows // 2
    direct = CHUNKS - SHARED
    dp = lax.axis_index("dp")
    ctx = lax.axis_index("ctx")
    x_at, y_at = dp % 2, dp // 2
    core = ctx % 2
    side = (ctx // 2) % 2
    to_x = {"dp": y_at * 2 + (1 - x_at)}
    to_y = {"dp": (1 - y_at) * 2 + x_at}
    to_core = {"ctx": ctx + 1 - 2 * core}
    to_z = {"ctx": ctx + 2 - 4 * side}
    owners = (dp, y_at * 2 + (1 - x_at), (1 - y_at) * 2 + x_at, (1 - y_at) * 2 + (1 - x_at))

    def place(i):
        at = i + side * (CHUNKS - 1 - 2 * i)
        return pl.ds(pl.multiple_of(at * rows + core * half, half), half)

    pairs = ((a_ref, big_a), (v_ref, big_v))

    def own_copy(way, i):
        target = to_x if way == 0 else to_y
        return [
            pltpu.make_async_remote_copy(
                src_ref=own.at[place(i)], dst_ref=big.at[way, place(i)],
                send_sem=send_sem.at[way, i, k], recv_sem=direct_sem.at[way, i, k],
                device_id=target, device_id_type=MESH)
            for k, (own, big) in enumerate(pairs)]

    def relay_copy(i):
        way = 0 if i % 2 else 1
        target = to_y if i % 2 else to_x
        return [
            pltpu.make_async_remote_copy(
                src_ref=big.at[way, place(i)], dst_ref=big.at[2, place(i)],
                send_sem=relay_sem.at[i, k], recv_sem=direct_sem.at[2, i, k],
                device_id=target, device_id_type=MESH)
            for k, (own, big) in enumerate(pairs)]

    def z_copy(way, i):
        return [
            pltpu.make_async_remote_copy(
                src_ref=big.at[way, place(i)], dst_ref=big.at[way, place(i)],
                send_sem=z_sem.at[way, i, k], recv_sem=direct_sem.at[way, CHUNKS - 1 - i, k],
                device_id=to_z, device_id_type=MESH)
            for k, (own, big) in enumerate(pairs)]

    def core_copy(way, i):
        return [
            pltpu.make_async_remote_copy(
                src_ref=big.at[way, place(i)], dst_ref=big.at[way, place(i)],
                send_sem=fwd_sem.at[way, i, k], recv_sem=core_sem.at[way, i, k],
                device_id=to_core, device_id_type=MESH)
            for k, (own, big) in enumerate(pairs)]

    started = []

    def start(copies):
        for copy in copies:
            copy.start()
            started.append(copy)

    def arrived(way, i):
        for k, (own, big) in enumerate(pairs):
            spot = big.at[way, place(i)]
            pltpu.make_async_copy(spot, spot, direct_sem.at[way, i, k]).wait()

    barrier = pltpu.get_barrier_semaphore()
    for target in (to_x, to_y, to_core, to_z):
        pl.semaphore_signal(barrier, inc=1, device_id=target, device_id_type=MESH)
    pl.semaphore_wait(barrier, 4)

    for i in range(2):
        start(own_copy(0, i))
        start(own_copy(1, i))

    own_at = pl.ds(pl.multiple_of(owners[0] * depth, depth), depth)
    tile = 512
    wide = acc_v.shape[1]
    acc_a[...] = jnp.dot(x_ref[:, own_at], a_ref[...], preferred_element_type=jnp.float32)

    def first(n, carry):
        cols = pl.ds(pl.multiple_of(n * tile, tile), tile)
        acc_v[:, cols] = jnp.dot(
            x_ref[:, own_at], v_ref[:, cols], preferred_element_type=jnp.float32)
        return carry

    lax.fori_loop(0, wide // tile, first, 0)

    def multiply(way, pair):
        span = 2 * rows
        at = pair + side * (CHUNKS // 2 - 1 - 2 * pair)
        low = pl.multiple_of(at * span, span)
        for i in (2 * pair, 2 * pair + 1):
            for k, (own, big) in enumerate(pairs):
                at_i = i + side * (CHUNKS - 1 - 2 * i)
                other = pl.ds(pl.multiple_of(at_i * rows + (1 - core) * half, half), half)
                spot = big.at[way, other]
                pltpu.make_async_copy(spot, spot, core_sem.at[way, i, k]).wait()
        part = x_ref[:, pl.ds(pl.multiple_of(owners[way + 1] * depth + low, span), span)]
        acc_a[...] += jnp.dot(
            part, big_a[way, pl.ds(low, span)], preferred_element_type=jnp.float32)

        def more(n, carry):
            cols = pl.ds(pl.multiple_of(n * tile, tile), tile)
            acc_v[:, cols] += jnp.dot(
                part, big_v[way, pl.ds(low, span), cols], preferred_element_type=jnp.float32)
            return carry

        lax.fori_loop(0, wide // tile, more, 0)

    ready = []

    def take(way, i):
        arrived(way, i)
        if i < SHARED:
            start(z_copy(way, i))
        if way < 2 and i < direct and way == (0 if i % 2 else 1):
            start(relay_copy(i))
        start(core_copy(way, i))

    seen = set()

    def note(way, i):
        take(way, i)
        seen.add((way, i))
        if (way, i ^ 1) in seen:
            ready.append((way, i // 2))

    lag = 2
    for step in range(direct + lag):
        if step < direct:
            note(0, step)
            note(1, step)
            if step + 2 < direct:
                start(own_copy(0, step + 2))
                start(own_copy(1, step + 2))
        if step >= lag:
            back = step - lag
            if back < SHARED:
                note(0, CHUNKS - 1 - back)
                note(1, CHUNKS - 1 - back)
            note(2, back)
        if step < direct and len(ready) > 1:
            multiply(*ready.pop(0))
    while len(ready) > 1:
        multiply(*ready.pop(0))
    for back in range(SHARED):
        note(2, CHUNKS - 1 - back)
    while ready:
        multiply(*ready.pop(0))
    for copy in started:
        copy.wait_send()
    narrow = qk_ref.shape[1]
    qk_ref[...] = acc_a[:, :narrow].astype(jnp.bfloat16)
    lam_ref[...] = jax.nn.softplus(acc_a[:, narrow:])
    val_ref[...] = acc_v[...].astype(jnp.bfloat16)


def project(tokens, query_weight, key_weight, value_weight, lambda_weight):
    length = tokens.shape[0]
    depth, wide = value_weight.shape
    narrow = query_weight.shape[1] + key_weight.shape[1]
    lams = lambda_weight.shape[1]
    fill = -lams % 128
    packed = jnp.concatenate(
        (query_weight, key_weight, lambda_weight, jnp.zeros((depth, fill), jnp.bfloat16)), axis=1)
    columns = packed.shape[1]
    vmem = pl.BlockSpec(memory_space=pltpu.VMEM)
    dma = pltpu.SemaphoreType.DMA
    return pl.pallas_call(
        gather_kernel,
        out_shape=(
            jax.ShapeDtypeStruct((length, narrow), jnp.bfloat16),
            jax.ShapeDtypeStruct((length, lams + fill), jnp.float32),
            jax.ShapeDtypeStruct((length, wide), jnp.bfloat16),
        ),
        in_specs=[vmem] * 3,
        out_specs=(vmem,) * 3,
        scratch_shapes=[
            pltpu.VMEM((3, depth, columns), jnp.bfloat16),
            pltpu.VMEM((3, depth, wide), jnp.bfloat16),
            pltpu.VMEM((length, columns), jnp.float32),
            pltpu.VMEM((length, wide), jnp.float32),
            dma((3, CHUNKS, 2)),
            dma((3, CHUNKS, 2)),
            dma((2, CHUNKS, 2)),
            dma((CHUNKS, 2)),
            dma((3, SHARED, 2)),
            dma((3, CHUNKS, 2)),
        ],
        compiler_params=pltpu.CompilerParams(
            collective_id=0, has_side_effects=True, vmem_limit_bytes=VMEM_LIMIT),
        name="gather_project",
    )(tokens, packed, value_weight)


def per_device(inputs, query_weight, key_weight, value_weight, lambda_weight, log_decay, norm_gain):
    tokens = inputs[0]
    decays = log_decay[0]
    length = tokens.shape[0]
    qk, lambdas, value_rows = project(
        tokens, query_weight, key_weight, value_weight, lambda_weight)
    state_dim = query_weight.shape[1]
    query_rows = qk[:, :state_dim]
    key_rows = qk[:, state_dim:]
    lambdas = lambdas[:, :lambda_weight.shape[1]]
    masks = level_masks(length)
    inner = masks.shape[0]
    scale = 1.0 / math.sqrt(query_rows.shape[1])
    near, state, total, cumulative, weights_all = block_terms(
        query_rows, key_rows, value_rows, lambdas, decays, masks
    )
    index = lax.axis_index("ctx")
    bits = lax.axis_size("ctx").bit_length() - 1
    block_state = state
    block_total = total
    carry_decay = jnp.ones_like(total)
    growth = jnp.exp(cumulative)
    mixed = near
    for level_bit in range(bits):
        other_state, other_total = from_partner(
            (block_state.astype(jnp.bfloat16), block_total), "ctx", level_bit)
        other_state = other_state.astype(jnp.float32)
        upper = (index >> level_bit & 1).astype(jnp.float32)
        carried = (carry_decay[:, None, None] * other_state).astype(jnp.bfloat16)
        reach = jnp.einsum("ts,hsd->thd", query_rows, carried, preferred_element_type=jnp.float32)
        factor = weights_all[:, :, inner + level_bit] * growth * (scale * upper)
        mixed = mixed + factor[..., None] * reach
        if level_bit + 1 < bits:
            block_state = jnp.where(
                upper > 0,
                block_total[:, None, None] * other_state + block_state,
                other_total[:, None, None] * block_state + other_state,
            )
            carry_decay = jnp.where(upper > 0, other_total * carry_decay, carry_decay)
            block_total = block_total * other_total
    return finish(mixed, norm_gain).reshape(1, length, -1)


def solution(mesh):
    return jax.shard_map(
        per_device,
        mesh=mesh,
        in_specs=(
            P("dp", "ctx", None),
            P("dp", None),
            P("dp", None),
            P("dp", None),
            P("dp", None),
            P("dp", "ctx", None),
            P(),
        ),
        out_specs=P("dp", "ctx", None),
        check_vma=False,
    )
```

```python
import functools
import math

import jax
import jax.numpy as jnp
from jax import lax
from jax.experimental import pallas as pl
from jax.experimental.pallas import tpu as pltpu
from jax.sharding import PartitionSpec as P

HIGHEST = lax.Precision.HIGHEST
MESH = pl.DeviceIdType.MESH
VMEM_LIMIT = 63 * 1024 * 1024


CHUNKS = 8
SHARED = 2


def gather_kernel(x_ref, a_ref, v_ref, qk_ref, lam_ref, val_ref, big_a, big_v, acc_a, acc_v,
                  direct_sem, core_sem, send_sem, relay_sem, z_sem, fwd_sem):
    depth = a_ref.shape[0]
    rows = depth // CHUNKS
    half = rows // 2
    direct = CHUNKS - SHARED
    dp = lax.axis_index("dp")
    ctx = lax.axis_index("ctx")
    x_at, y_at = dp % 2, dp // 2
    core = ctx % 2
    side = (ctx // 2) % 2
    to_x = {"dp": y_at * 2 + (1 - x_at)}
    to_y = {"dp": (1 - y_at) * 2 + x_at}
    to_core = {"ctx": ctx + 1 - 2 * core}
    to_z = {"ctx": ctx + 2 - 4 * side}
    owners = (dp, y_at * 2 + (1 - x_at), (1 - y_at) * 2 + x_at, (1 - y_at) * 2 + (1 - x_at))

    def place(i):
        at = i + side * (CHUNKS - 1 - 2 * i)
        return pl.ds(pl.multiple_of(at * rows + core * half, half), half)

    pairs = ((a_ref, big_a), (v_ref, big_v))

    def own_copy(way, i):
        target = to_x if way == 0 else to_y
        return [
            pltpu.make_async_remote_copy(
                src_ref=own.at[place(i)], dst_ref=big.at[way, place(i)],
                send_sem=send_sem.at[way, i, k], recv_sem=direct_sem.at[way, i, k],
                device_id=target, device_id_type=MESH)
            for k, (own, big) in enumerate(pairs)]

    def relay_copy(i):
        way = 0 if i % 2 else 1
        target = to_y if i % 2 else to_x
        return [
            pltpu.make_async_remote_copy(
                src_ref=big.at[way, place(i)], dst_ref=big.at[2, place(i)],
                send_sem=relay_sem.at[i, k], recv_sem=direct_sem.at[2, i, k],
                device_id=target, device_id_type=MESH)
            for k, (own, big) in enumerate(pairs)]

    def z_copy(way, i):
        return [
            pltpu.make_async_remote_copy(
                src_ref=big.at[way, place(i)], dst_ref=big.at[way, place(i)],
                send_sem=z_sem.at[way, i, k], recv_sem=direct_sem.at[way, CHUNKS - 1 - i, k],
                device_id=to_z, device_id_type=MESH)
            for k, (own, big) in enumerate(pairs)]

    def core_copy(way, i):
        return [
            pltpu.make_async_remote_copy(
                src_ref=big.at[way, place(i)], dst_ref=big.at[way, place(i)],
                send_sem=fwd_sem.at[way, i, k], recv_sem=core_sem.at[way, i, k],
                device_id=to_core, device_id_type=MESH)
            for k, (own, big) in enumerate(pairs)]

    started = []

    def start(copies):
        for copy in copies:
            copy.start()
            started.append(copy)

    def arrived(way, i):
        for k, (own, big) in enumerate(pairs):
            spot = big.at[way, place(i)]
            pltpu.make_async_copy(spot, spot, direct_sem.at[way, i, k]).wait()

    barrier = pltpu.get_barrier_semaphore()
    for target in (to_x, to_y, to_core, to_z):
        pl.semaphore_signal(barrier, inc=1, device_id=target, device_id_type=MESH)
    pl.semaphore_wait(barrier, 4)

    for i in range(2):
        start(own_copy(0, i))
        start(own_copy(1, i))

    own_at = pl.ds(pl.multiple_of(owners[0] * depth, depth), depth)
    tile = 512
    wide = acc_v.shape[1]
    acc_a[...] = jnp.dot(x_ref[:, own_at], a_ref[...], preferred_element_type=jnp.float32)

    def first(n, carry):
        cols = pl.ds(pl.multiple_of(n * tile, tile), tile)
        acc_v[:, cols] = jnp.dot(
            x_ref[:, own_at], v_ref[:, cols], preferred_element_type=jnp.float32)
        return carry

    lax.fori_loop(0, wide // tile, first, 0)

    def multiply(way, pair):
        span = 2 * rows
        at = pair + side * (CHUNKS // 2 - 1 - 2 * pair)
        low = pl.multiple_of(at * span, span)
        for i in (2 * pair, 2 * pair + 1):
            for k, (own, big) in enumerate(pairs):
                at_i = i + side * (CHUNKS - 1 - 2 * i)
                other = pl.ds(pl.multiple_of(at_i * rows + (1 - core) * half, half), half)
                spot = big.at[way, other]
                pltpu.make_async_copy(spot, spot, core_sem.at[way, i, k]).wait()
        part = x_ref[:, pl.ds(pl.multiple_of(owners[way + 1] * depth + low, span), span)]
        acc_a[...] += jnp.dot(
            part, big_a[way, pl.ds(low, span)], preferred_element_type=jnp.float32)

        def more(n, carry):
            cols = pl.ds(pl.multiple_of(n * tile, tile), tile)
            acc_v[:, cols] += jnp.dot(
                part, big_v[way, pl.ds(low, span), cols], preferred_element_type=jnp.float32)
            return carry

        lax.fori_loop(0, wide // tile, more, 0)

    ready = []

    def take(way, i):
        arrived(way, i)
        if i < SHARED:
            start(z_copy(way, i))
        if way < 2 and i < direct and way == (0 if i % 2 else 1):
            start(relay_copy(i))
        start(core_copy(way, i))

    seen = set()

    def note(way, i):
        take(way, i)
        seen.add((way, i))
        if (way, i ^ 1) in seen:
            ready.append((way, i // 2))

    lag = 2
    for step in range(direct + lag):
        if step < direct:
            note(0, step)
            note(1, step)
            if step + 2 < direct:
                start(own_copy(0, step + 2))
                start(own_copy(1, step + 2))
        if step >= lag:
            back = step - lag
            if back < SHARED:
                note(0, CHUNKS - 1 - back)
                note(1, CHUNKS - 1 - back)
            note(2, back)
        if step < direct and len(ready) > 1:
            multiply(*ready.pop(0))
    while len(ready) > 1:
        multiply(*ready.pop(0))
    for back in range(SHARED):
        note(2, CHUNKS - 1 - back)
    while ready:
        multiply(*ready.pop(0))
    for copy in started:
        copy.wait_send()
    narrow = qk_ref.shape[1]
    qk_ref[...] = acc_a[:, :narrow].astype(jnp.bfloat16)
    lam_ref[...] = jax.nn.softplus(acc_a[:, narrow:])
    val_ref[...] = acc_v[...].astype(jnp.bfloat16)


def project(tokens, query_weight, key_weight, value_weight, lambda_weight):
    length = tokens.shape[0]
    depth, wide = value_weight.shape
    narrow = query_weight.shape[1] + key_weight.shape[1]
    lams = lambda_weight.shape[1]
    fill = -lams % 128
    packed = jnp.concatenate(
        (query_weight, key_weight, lambda_weight, jnp.zeros((depth, fill), jnp.bfloat16)), axis=1)
    columns = packed.shape[1]
    vmem = pl.BlockSpec(memory_space=pltpu.VMEM)
    dma = pltpu.SemaphoreType.DMA
    return pl.pallas_call(
        gather_kernel,
        out_shape=(
            jax.ShapeDtypeStruct((length, narrow), jnp.bfloat16),
            jax.ShapeDtypeStruct((length, lams + fill), jnp.float32),
            jax.ShapeDtypeStruct((length, wide), jnp.bfloat16),
        ),
        in_specs=[vmem] * 3,
        out_specs=(vmem,) * 3,
        scratch_shapes=[
            pltpu.VMEM((3, depth, columns), jnp.bfloat16),
            pltpu.VMEM((3, depth, wide), jnp.bfloat16),
            pltpu.VMEM((length, columns), jnp.float32),
            pltpu.VMEM((length, wide), jnp.float32),
            dma((3, CHUNKS, 2)),
            dma((3, CHUNKS, 2)),
            dma((2, CHUNKS, 2)),
            dma((CHUNKS, 2)),
            dma((3, SHARED, 2)),
            dma((3, CHUNKS, 2)),
        ],
        compiler_params=pltpu.CompilerParams(
            collective_id=0, has_side_effects=True, vmem_limit_bytes=VMEM_LIMIT),
        name="gather_project",
    )(tokens, packed, value_weight)


def flipped(index, mask):
    out = index
    for power in range(mask.bit_length()):
        if mask >> power & 1:
            step = 1 << power
            out = out + step - 2 * step * ((index // step) % 2)
    return out


def mixer_kernel(levels, qk_ref, lam_ref, val_ref, decay_ref, gain_ref, out_ref, logs, state,
                 sent, got, mixed, score, cum, grow, log_send, log_recv, first_send, first_recv,
                 part_send, part_recv, share_send, share_recv):
    count = lax.axis_size("ctx")
    bits = count.bit_length() - 1
    ctx = lax.axis_index("ctx")
    length, heads = decay_ref.shape
    head_dim = val_ref.shape[1] // heads
    state_dim = qk_ref.shape[1] // 2
    inner = length.bit_length()
    scale = 1.0 / math.sqrt(state_dim)
    tile = 128
    tiles = length // tile
    peers = [None] + [{"ctx": flipped(ctx, r)} for r in range(1, count)]
    started = []

    def send(src, dst, out_sem, in_sem, peer):
        copy = pltpu.make_async_remote_copy(
            src_ref=src, dst_ref=dst, send_sem=out_sem, recv_sem=in_sem,
            device_id=peers[peer], device_id_type=MESH)
        copy.start()
        started.append(copy)

    def await_at(spot, sem):
        pltpu.make_async_copy(spot, spot, sem).wait()

    barrier = pltpu.get_barrier_semaphore()
    for r in range(1, count):
        pl.semaphore_signal(barrier, inc=1, device_id=peers[r], device_id_type=MESH)

    row = lax.broadcasted_iota(jnp.int32, (length, length), 0)
    col = lax.broadcasted_iota(jnp.int32, (length, length), 1)
    below = (row >= col).astype(jnp.float32)
    decays = decay_ref[...]
    ones = jnp.ones((length, tile), jnp.float32)
    logs[0] = lax.dot_general(
        decays, ones, (((0,), (0,)), ((), ())), precision=HIGHEST,
        preferred_element_type=jnp.float32)
    cum_col = jnp.dot(below, decays, precision=HIGHEST, preferred_element_type=jnp.float32)
    cum_row = lax.dot_general(
        decays, below, (((0,), (1,)), ((), ())), precision=HIGHEST,
        preferred_element_type=jnp.float32)
    cum[...] = cum_row
    grow[...] = jnp.exp(cum_col) * scale
    remain = jnp.exp(cum_col[length - 1:length] - cum_col)
    pl.semaphore_wait(barrier, count - 1)
    for r in range(1, count):
        send(logs.at[0], logs.at[r], log_send.at[r], log_recv.at[r], r)

    def values_of(h):
        return val_ref[:, h * head_dim:(h + 1) * head_dim]

    keys = qk_ref[:, state_dim:].astype(jnp.float32)
    halves = 2
    for part in range(halves):
        span = heads // halves
        for h in range(part * span, (part + 1) * span):
            keyed = (keys * remain[:, h:h + 1]).astype(jnp.bfloat16)
            block = lax.dot_general(
                keyed, values_of(h), (((0,), (0,)), ((), ())),
                preferred_element_type=jnp.float32)
            state[h] = block
            sent[0, h] = block.astype(jnp.bfloat16)
        if bits > 0:
            at = pl.ds(part * span, span)
            send(sent.at[0, at], got.at[0, at], first_send.at[part], first_recv.at[part], 1)

    trow = lax.broadcasted_iota(jnp.int32, (tile, tile), 0)
    tcol = lax.broadcasted_iota(jnp.int32, (tile, tile), 1)
    differ = jnp.bitwise_xor(trow, tcol)
    depth = tile.bit_length() - 1
    full = lax.dot_general(
        qk_ref[:, :state_dim], qk_ref[:, state_dim:], (((1,), (1,)), ((), ())),
        preferred_element_type=jnp.float32)
    score[...] = jnp.where(row >= col, full * scale, 0.0)

    def near(h):
        base = h * levels
        for ti in range(tiles):
            rows = slice(ti * tile, (ti + 1) * tile)
            total = None
            for tj in range(ti + 1):
                cols = slice(tj * tile, (tj + 1) * tile)
                if ti == tj:
                    weight = jnp.broadcast_to(lam_ref[rows, base:base + 1], (tile, tile))
                    for level in range(1, depth + 1):
                        at = base + level
                        weight = jnp.where(
                            differ >= 1 << (level - 1), lam_ref[rows, at:at + 1], weight)
                else:
                    at = base + depth + (ti ^ tj).bit_length()
                    weight = lam_ref[rows, at:at + 1]
                distance = cum_col[rows, h:h + 1] - cum[h:h + 1, cols]
                decay = jnp.exp(jnp.minimum(distance, 0.0))
                mix = (weight * (decay * score[rows, cols])).astype(jnp.bfloat16)
                term = jnp.dot(
                    mix, val_ref[cols, h * head_dim:(h + 1) * head_dim],
                    preferred_element_type=jnp.float32)
                total = term if total is None else total + term
            mixed[rows, h * head_dim:(h + 1) * head_dim] = total

    left = list(range(heads))

    def near_some(most):
        for _ in range(min(most, len(left))):
            near(left.pop(0))

    def far(b, h, carry, upper):
        carried = (carry[h:h + 1] * got[b, h].astype(jnp.float32)).astype(jnp.bfloat16)
        reach = jnp.dot(qk_ref[:, :state_dim], carried, preferred_element_type=jnp.float32)
        at = h * levels + inner + b
        factor = lam_ref[:, at:at + 1] * grow[:, h:h + 1] * upper
        return factor * reach

    near_some(3)
    for r in range(1, count):
        await_at(logs.at[r], log_recv.at[r])
    own_log = logs[0]
    carry_log = jnp.zeros_like(own_log)
    pending = []
    for b in range(bits):
        upper = ((ctx // (1 << b)) % 2).astype(jnp.float32)
        other_log = logs[1 << b]
        for r in range((1 << b) + 1, 2 << b):
            other_log = other_log + logs[r]
        group = min(1 << b, 4)
        if b == 0:
            for part in range(halves):
                at = pl.ds(part * (heads // halves), heads // halves)
                await_at(got.at[0, at], first_recv.at[part])
        else:
            span = heads // group

            def slot(ref, r):
                return ref.at[b, pl.ds(flipped(ctx % group, r) * span, span)]

            await_at(slot(got, 0), part_recv.at[b])
            for r in range(1, group):
                send(slot(got, 0), slot(got, 0), share_send.at[b, r], share_recv.at[b, r], r)
            near_some(2)
            if b + 1 == bits:
                near_some(heads)
                for p in pending:
                    for h in range(heads):
                        cols = slice(h * head_dim, (h + 1) * head_dim)
                        mixed[:, cols] += far(p[0], h, p[1], p[2])
            for r in range(1, group):
                await_at(slot(got, r), share_recv.at[b, r])
        pending.append((b, jnp.exp(carry_log), upper))
        if b + 1 < bits:
            keep = jnp.where(upper > 0, 1.0, jnp.exp(other_log))
            take = jnp.where(upper > 0, jnp.exp(own_log), 1.0)
            for h in range(heads):
                block = keep[h:h + 1] * state[h] + take[h:h + 1] * got[b, h].astype(jnp.float32)
                state[h] = block
                sent[b + 1, h] = block.astype(jnp.bfloat16)
            ahead = min(2 << b, 4)
            wide = heads // ahead
            at = pl.ds((ctx % ahead) * wide, wide)
            send(sent.at[b + 1, at], got.at[b + 1, at], part_send.at[b + 1],
                 part_recv.at[b + 1], 2 << b)
            carry_log = carry_log + upper * other_log
            own_log = own_log + other_log
            near_some(5)
    near_some(heads)
    rest = pending[-1:] if bits > 1 else pending
    for h in range(heads):
        cols = slice(h * head_dim, (h + 1) * head_dim)
        whole = mixed[:, cols]
        for p in rest:
            whole = whole + far(p[0], h, p[1], p[2])
        mean_square = jnp.mean(whole * whole, axis=-1, keepdims=True)
        out_ref[:, cols] = (whole * lax.rsqrt(mean_square + 1e-05) * gain_ref[:, cols]).astype(
            jnp.bfloat16)
    for copy in started:
        copy.wait_send()


def mix_all(qk, lambdas, value_rows, decays, norm_gain, levels):
    length, heads = decays.shape
    wide = value_rows.shape[1]
    state_dim = qk.shape[1] // 2
    head_dim = wide // heads
    count = lax.axis_size("ctx")
    bits = count.bit_length() - 1
    vmem = pl.BlockSpec(memory_space=pltpu.VMEM)
    dma = pltpu.SemaphoreType.DMA
    return pl.pallas_call(
        functools.partial(mixer_kernel, levels),
        out_shape=jax.ShapeDtypeStruct((length, wide), jnp.bfloat16),
        in_specs=[vmem] * 5,
        out_specs=vmem,
        scratch_shapes=[
            pltpu.VMEM((count, heads, 128), jnp.float32),
            pltpu.VMEM((heads, state_dim, head_dim), jnp.float32),
            pltpu.VMEM((bits, heads, state_dim, head_dim), jnp.bfloat16),
            pltpu.VMEM((bits, heads, state_dim, head_dim), jnp.bfloat16),
            pltpu.VMEM((length, wide), jnp.float32),
            pltpu.VMEM((length, length), jnp.float32),
            pltpu.VMEM((heads, length), jnp.float32),
            pltpu.VMEM((length, heads), jnp.float32),
            dma((count,)),
            dma((count,)),
            dma((2,)),
            dma((2,)),
            dma((bits,)),
            dma((bits,)),
            dma((bits, 4)),
            dma((bits, 4)),
        ],
        compiler_params=pltpu.CompilerParams(
            collective_id=1, has_side_effects=True, vmem_limit_bytes=VMEM_LIMIT),
        name="mixer",
    )(qk, lambdas, value_rows, decays, norm_gain[None])


def per_device(inputs, query_weight, key_weight, value_weight, lambda_weight, log_decay, norm_gain):
    qk, lambdas, value_rows = project(
        inputs[0], query_weight, key_weight, value_weight, lambda_weight)
    levels = lambda_weight.shape[1] // log_decay.shape[2]
    return mix_all(qk, lambdas, value_rows, log_decay[0], norm_gain, levels)[None]


def solution(mesh):
    return jax.shard_map(
        per_device,
        mesh=mesh,
        in_specs=(
            P("dp", "ctx", None),
            P("dp", None),
            P("dp", None),
            P("dp", None),
            P("dp", None),
            P("dp", "ctx", None),
            P(),
        ),
        out_specs=P("dp", "ctx", None),
        check_vma=False,
    )
```

```python
import functools
import math

import jax
import jax.numpy as jnp
from jax import lax
from jax.experimental import pallas as pl
from jax.experimental.pallas import tpu as pltpu
from jax.sharding import PartitionSpec as P

HIGHEST = lax.Precision.HIGHEST
MESH = pl.DeviceIdType.MESH
VMEM_LIMIT = 63 * 1024 * 1024


CHUNKS = 16
SHARED = 5
PACK = 4


def gather_kernel(x_ref, a_ref, v_ref, qk_ref, lam_ref, val_ref, big_a, big_v, acc_a, acc_v,
                  direct_sem, core_sem, send_sem, relay_sem, z_sem, fwd_sem):
    depth = a_ref.shape[0]
    rows = depth // CHUNKS
    half = rows // 2
    direct = CHUNKS - SHARED
    dp = lax.axis_index("dp")
    ctx = lax.axis_index("ctx")
    x_at, y_at = dp % 2, dp // 2
    core = ctx % 2
    side = (ctx // 2) % 2
    to_x = {"dp": y_at * 2 + (1 - x_at)}
    to_y = {"dp": (1 - y_at) * 2 + x_at}
    to_core = {"ctx": ctx + 1 - 2 * core}
    to_z = {"ctx": ctx + 2 - 4 * side}
    owners = (dp, y_at * 2 + (1 - x_at), (1 - y_at) * 2 + x_at, (1 - y_at) * 2 + (1 - x_at))

    def place(i):
        at = i + side * (CHUNKS - 1 - 2 * i)
        return pl.ds(pl.multiple_of(at * rows + core * half, half), half)

    pairs = ((a_ref, big_a), (v_ref, big_v))

    def own_copy(way, i):
        target = to_x if way == 0 else to_y
        return [
            pltpu.make_async_remote_copy(
                src_ref=own.at[place(i)], dst_ref=big.at[way, place(i)],
                send_sem=send_sem.at[way, i, k], recv_sem=direct_sem.at[way, i, k],
                device_id=target, device_id_type=MESH)
            for k, (own, big) in enumerate(pairs)]

    def relay_copy(i):
        way = 0 if i % 2 else 1
        target = to_y if i % 2 else to_x
        return [
            pltpu.make_async_remote_copy(
                src_ref=big.at[way, place(i)], dst_ref=big.at[2, place(i)],
                send_sem=relay_sem.at[i, k], recv_sem=direct_sem.at[2, i, k],
                device_id=target, device_id_type=MESH)
            for k, (own, big) in enumerate(pairs)]

    def z_copy(way, i):
        return [
            pltpu.make_async_remote_copy(
                src_ref=big.at[way, place(i)], dst_ref=big.at[way, place(i)],
                send_sem=z_sem.at[way, i, k], recv_sem=direct_sem.at[way, CHUNKS - 1 - i, k],
                device_id=to_z, device_id_type=MESH)
            for k, (own, big) in enumerate(pairs)]

    def core_copy(way, i):
        return [
            pltpu.make_async_remote_copy(
                src_ref=big.at[way, place(i)], dst_ref=big.at[way, place(i)],
                send_sem=fwd_sem.at[way, i, k], recv_sem=core_sem.at[way, i, k],
                device_id=to_core, device_id_type=MESH)
            for k, (own, big) in enumerate(pairs)]

    started = []

    def start(copies):
        for copy in copies:
            copy.start()
            started.append(copy)

    def arrived(way, i):
        for k, (own, big) in enumerate(pairs):
            spot = big.at[way, place(i)]
            pltpu.make_async_copy(spot, spot, direct_sem.at[way, i, k]).wait()

    barrier = pltpu.get_barrier_semaphore()
    for target in (to_x, to_y, to_core, to_z):
        pl.semaphore_signal(barrier, inc=1, device_id=target, device_id_type=MESH)
    pl.semaphore_wait(barrier, 4)

    for i in range(2):
        start(own_copy(0, i))
        start(own_copy(1, i))

    own_at = pl.ds(pl.multiple_of(owners[0] * depth, depth), depth)
    tile = 512
    wide = acc_v.shape[1]
    acc_a[...] = jnp.dot(x_ref[:, own_at], a_ref[...], preferred_element_type=jnp.float32)

    def first(n, carry):
        cols = pl.ds(pl.multiple_of(n * tile, tile), tile)
        acc_v[:, cols] = jnp.dot(
            x_ref[:, own_at], v_ref[:, cols], preferred_element_type=jnp.float32)
        return carry

    lax.fori_loop(0, wide // tile, first, 0)

    def multiply(way, pack):
        span = PACK * rows
        at = pack + side * (CHUNKS // PACK - 1 - 2 * pack)
        low = pl.multiple_of(at * span, span)
        for i in range(PACK * pack, PACK * (pack + 1)):
            for k, (own, big) in enumerate(pairs):
                at_i = i + side * (CHUNKS - 1 - 2 * i)
                other = pl.ds(pl.multiple_of(at_i * rows + (1 - core) * half, half), half)
                spot = big.at[way, other]
                pltpu.make_async_copy(spot, spot, core_sem.at[way, i, k]).wait()
        part = x_ref[:, pl.ds(pl.multiple_of(owners[way + 1] * depth + low, span), span)]
        acc_a[...] += jnp.dot(
            part, big_a[way, pl.ds(low, span)], preferred_element_type=jnp.float32)

        def more(n, carry):
            cols = pl.ds(pl.multiple_of(n * tile, tile), tile)
            acc_v[:, cols] += jnp.dot(
                part, big_v[way, pl.ds(low, span), cols], preferred_element_type=jnp.float32)
            return carry

        lax.fori_loop(0, wide // tile, more, 0)

    ready = []

    def take(way, i):
        arrived(way, i)
        if i < SHARED:
            start(z_copy(way, i))
        if way < 2 and i < direct and way == (0 if i % 2 else 1):
            start(relay_copy(i))
        start(core_copy(way, i))

    seen = {}

    def note(way, i):
        take(way, i)
        pack = (way, i // PACK)
        seen[pack] = seen.get(pack, 0) + 1
        if seen[pack] == PACK:
            ready.append(pack)

    lag = 2
    crossed = []
    for step in range(SHARED + lag):
        crossed += [(way, step) for way in range(2) if step < SHARED]
        crossed += [(2, step - lag)] if step >= lag else []
    taken = 0
    for step in range(direct + lag):
        due, ready[:] = list(ready), []
        if step < direct:
            note(0, step)
            note(1, step)
            if step + 2 < direct:
                start(own_copy(0, step + 2))
                start(own_copy(1, step + 2))
        if step >= lag:
            note(2, step - lag)
        while taken < min(len(crossed), (3 * step - 1) // 2):
            way, i = crossed[taken]
            note(way, CHUNKS - 1 - i)
            taken += 1
        for pack in due:
            multiply(*pack)
    while taken < len(crossed):
        way, i = crossed[taken]
        note(way, CHUNKS - 1 - i)
        taken += 1
    while ready:
        multiply(*ready.pop(0))
    for copy in started:
        copy.wait_send()
    narrow = qk_ref.shape[1]
    qk_ref[...] = acc_a[:, :narrow].astype(jnp.bfloat16)
    lam_ref[...] = jax.nn.softplus(acc_a[:, narrow:])
    val_ref[...] = acc_v[...].astype(jnp.bfloat16)


def project(tokens, query_weight, key_weight, value_weight, lambda_weight):
    length = tokens.shape[0]
    depth, wide = value_weight.shape
    narrow = query_weight.shape[1] + key_weight.shape[1]
    lams = lambda_weight.shape[1]
    fill = -lams % 128
    packed = jnp.concatenate(
        (query_weight, key_weight, lambda_weight, jnp.zeros((depth, fill), jnp.bfloat16)), axis=1)
    columns = packed.shape[1]
    vmem = pl.BlockSpec(memory_space=pltpu.VMEM)
    dma = pltpu.SemaphoreType.DMA
    return pl.pallas_call(
        gather_kernel,
        out_shape=(
            jax.ShapeDtypeStruct((length, narrow), jnp.bfloat16),
            jax.ShapeDtypeStruct((length, lams + fill), jnp.float32),
            jax.ShapeDtypeStruct((length, wide), jnp.bfloat16),
        ),
        in_specs=[vmem] * 3,
        out_specs=(vmem,) * 3,
        scratch_shapes=[
            pltpu.VMEM((3, depth, columns), jnp.bfloat16),
            pltpu.VMEM((3, depth, wide), jnp.bfloat16),
            pltpu.VMEM((length, columns), jnp.float32),
            pltpu.VMEM((length, wide), jnp.float32),
            dma((3, CHUNKS, 2)),
            dma((3, CHUNKS, 2)),
            dma((2, CHUNKS, 2)),
            dma((CHUNKS, 2)),
            dma((3, SHARED, 2)),
            dma((3, CHUNKS, 2)),
        ],
        compiler_params=pltpu.CompilerParams(
            collective_id=0, has_side_effects=True, vmem_limit_bytes=VMEM_LIMIT),
        name="gather_project",
    )(tokens, packed, value_weight)


def flipped(index, mask):
    out = index
    for power in range(mask.bit_length()):
        if mask >> power & 1:
            step = 1 << power
            out = out + step - 2 * step * ((index // step) % 2)
    return out


def mixer_kernel(levels, qk_ref, lam_ref, val_ref, decay_ref, gain_ref, out_ref, logs, state,
                 sent, got, mixed, score, cum, grow, log_send, log_recv, first_send, first_recv,
                 part_send, part_recv, share_send, share_recv):
    count = lax.axis_size("ctx")
    bits = count.bit_length() - 1
    ctx = lax.axis_index("ctx")
    length, heads = decay_ref.shape
    head_dim = val_ref.shape[1] // heads
    state_dim = qk_ref.shape[1] // 2
    inner = length.bit_length()
    scale = 1.0 / math.sqrt(state_dim)
    tile = 128
    tiles = length // tile
    peers = [None] + [{"ctx": flipped(ctx, r)} for r in range(1, count)]
    started = []

    def send(src, dst, out_sem, in_sem, peer):
        copy = pltpu.make_async_remote_copy(
            src_ref=src, dst_ref=dst, send_sem=out_sem, recv_sem=in_sem,
            device_id=peers[peer], device_id_type=MESH)
        copy.start()
        started.append(copy)

    def await_at(spot, sem):
        pltpu.make_async_copy(spot, spot, sem).wait()

    barrier = pltpu.get_barrier_semaphore()
    for r in range(1, count):
        pl.semaphore_signal(barrier, inc=1, device_id=peers[r], device_id_type=MESH)

    row = lax.broadcasted_iota(jnp.int32, (length, length), 0)
    col = lax.broadcasted_iota(jnp.int32, (length, length), 1)
    below = (row >= col).astype(jnp.float32)
    decays = decay_ref[...]
    ones = jnp.ones((length, tile), jnp.float32)
    logs[0] = lax.dot_general(
        decays, ones, (((0,), (0,)), ((), ())), precision=HIGHEST,
        preferred_element_type=jnp.float32)
    cum_col = jnp.dot(below, decays, precision=HIGHEST, preferred_element_type=jnp.float32)
    cum_row = lax.dot_general(
        decays, below, (((0,), (1,)), ((), ())), precision=HIGHEST,
        preferred_element_type=jnp.float32)
    cum[...] = cum_row
    grow[...] = jnp.exp(cum_col) * scale
    remain = jnp.exp(cum_col[length - 1:length] - cum_col)
    pl.semaphore_wait(barrier, count - 1)
    for r in range(1, count):
        send(logs.at[0], logs.at[r], log_send.at[r], log_recv.at[r], r)

    def values_of(h):
        return val_ref[:, h * head_dim:(h + 1) * head_dim]

    keys = qk_ref[:, state_dim:].astype(jnp.float32)
    halves = 2
    for part in range(halves):
        span = heads // halves
        for h in range(part * span, (part + 1) * span):
            keyed = (keys * remain[:, h:h + 1]).astype(jnp.bfloat16)
            block = lax.dot_general(
                keyed, values_of(h), (((0,), (0,)), ((), ())),
                preferred_element_type=jnp.float32)
            state[h] = block
            sent[0, h] = block.astype(jnp.bfloat16)
        if bits > 0:
            at = pl.ds(part * span, span)
            send(sent.at[0, at], got.at[0, at], first_send.at[part], first_recv.at[part], 1)

    trow = lax.broadcasted_iota(jnp.int32, (tile, tile), 0)
    tcol = lax.broadcasted_iota(jnp.int32, (tile, tile), 1)
    differ = jnp.bitwise_xor(trow, tcol)
    depth = tile.bit_length() - 1
    full = lax.dot_general(
        qk_ref[:, :state_dim], qk_ref[:, state_dim:], (((1,), (1,)), ((), ())),
        preferred_element_type=jnp.float32)
    score[...] = jnp.where(row >= col, full * scale, 0.0)

    def near(h):
        base = h * levels
        for ti in range(tiles):
            rows = slice(ti * tile, (ti + 1) * tile)
            total = None
            for tj in range(ti + 1):
                cols = slice(tj * tile, (tj + 1) * tile)
                if ti == tj:
                    weight = jnp.broadcast_to(lam_ref[rows, base:base + 1], (tile, tile))
                    for level in range(1, depth + 1):
                        at = base + level
                        weight = jnp.where(
                            differ >= 1 << (level - 1), lam_ref[rows, at:at + 1], weight)
                else:
                    at = base + depth + (ti ^ tj).bit_length()
                    weight = lam_ref[rows, at:at + 1]
                distance = cum_col[rows, h:h + 1] - cum[h:h + 1, cols]
                decay = jnp.exp(jnp.minimum(distance, 0.0))
                mix = (weight * (decay * score[rows, cols])).astype(jnp.bfloat16)
                term = jnp.dot(
                    mix, val_ref[cols, h * head_dim:(h + 1) * head_dim],
                    preferred_element_type=jnp.float32)
                total = term if total is None else total + term
            mixed[rows, h * head_dim:(h + 1) * head_dim] = total

    left = list(range(heads))

    def near_some(most):
        for _ in range(min(most, len(left))):
            near(left.pop(0))

    def far(b, h, carry, upper):
        carried = (carry[h:h + 1] * got[b, h].astype(jnp.float32)).astype(jnp.bfloat16)
        reach = jnp.dot(qk_ref[:, :state_dim], carried, preferred_element_type=jnp.float32)
        at = h * levels + inner + b
        factor = lam_ref[:, at:at + 1] * grow[:, h:h + 1] * upper
        return factor * reach

    near_some(3)
    for r in range(1, count):
        await_at(logs.at[r], log_recv.at[r])
    own_log = logs[0]
    carry_log = jnp.zeros_like(own_log)
    pending = []
    for b in range(bits):
        upper = ((ctx // (1 << b)) % 2).astype(jnp.float32)
        other_log = logs[1 << b]
        for r in range((1 << b) + 1, 2 << b):
            other_log = other_log + logs[r]
        group = min(1 << b, 4)
        if b == 0:
            for part in range(halves):
                at = pl.ds(part * (heads // halves), heads // halves)
                await_at(got.at[0, at], first_recv.at[part])
        else:
            span = heads // group

            def slot(ref, r):
                return ref.at[b, pl.ds(flipped(ctx % group, r) * span, span)]

            await_at(slot(got, 0), part_recv.at[b])
            for r in range(1, group):
                send(slot(got, 0), slot(got, 0), share_send.at[b, r], share_recv.at[b, r], r)
            near_some(2)
            if b + 1 == bits:
                near_some(heads)
                for p in pending:
                    for h in range(heads):
                        cols = slice(h * head_dim, (h + 1) * head_dim)
                        mixed[:, cols] += far(p[0], h, p[1], p[2])
            for r in range(1, group):
                await_at(slot(got, r), share_recv.at[b, r])
        pending.append((b, jnp.exp(carry_log), upper))
        if b + 1 < bits:
            keep = jnp.where(upper > 0, 1.0, jnp.exp(other_log))
            take = jnp.where(upper > 0, jnp.exp(own_log), 1.0)
            for h in range(heads):
                block = keep[h:h + 1] * state[h] + take[h:h + 1] * got[b, h].astype(jnp.float32)
                state[h] = block
                sent[b + 1, h] = block.astype(jnp.bfloat16)
            ahead = min(2 << b, 4)
            wide = heads // ahead
            at = pl.ds((ctx % ahead) * wide, wide)
            send(sent.at[b + 1, at], got.at[b + 1, at], part_send.at[b + 1],
                 part_recv.at[b + 1], 2 << b)
            carry_log = carry_log + upper * other_log
            own_log = own_log + other_log
            near_some(5)
    near_some(heads)
    rest = pending[-1:] if bits > 1 else pending
    for h in range(heads):
        cols = slice(h * head_dim, (h + 1) * head_dim)
        whole = mixed[:, cols]
        for p in rest:
            whole = whole + far(p[0], h, p[1], p[2])
        mean_square = jnp.mean(whole * whole, axis=-1, keepdims=True)
        out_ref[:, cols] = (whole * lax.rsqrt(mean_square + 1e-05) * gain_ref[:, cols]).astype(
            jnp.bfloat16)
    for copy in started:
        copy.wait_send()


def mix_all(qk, lambdas, value_rows, decays, norm_gain, levels):
    length, heads = decays.shape
    wide = value_rows.shape[1]
    state_dim = qk.shape[1] // 2
    head_dim = wide // heads
    count = lax.axis_size("ctx")
    bits = count.bit_length() - 1
    vmem = pl.BlockSpec(memory_space=pltpu.VMEM)
    dma = pltpu.SemaphoreType.DMA
    return pl.pallas_call(
        functools.partial(mixer_kernel, levels),
        out_shape=jax.ShapeDtypeStruct((length, wide), jnp.bfloat16),
        in_specs=[vmem] * 5,
        out_specs=vmem,
        scratch_shapes=[
            pltpu.VMEM((count, heads, 128), jnp.float32),
            pltpu.VMEM((heads, state_dim, head_dim), jnp.float32),
            pltpu.VMEM((bits, heads, state_dim, head_dim), jnp.bfloat16),
            pltpu.VMEM((bits, heads, state_dim, head_dim), jnp.bfloat16),
            pltpu.VMEM((length, wide), jnp.float32),
            pltpu.VMEM((length, length), jnp.float32),
            pltpu.VMEM((heads, length), jnp.float32),
            pltpu.VMEM((length, heads), jnp.float32),
            dma((count,)),
            dma((count,)),
            dma((2,)),
            dma((2,)),
            dma((bits,)),
            dma((bits,)),
            dma((bits, 4)),
            dma((bits, 4)),
        ],
        compiler_params=pltpu.CompilerParams(
            collective_id=1, has_side_effects=True, vmem_limit_bytes=VMEM_LIMIT),
        name="mixer",
    )(qk, lambdas, value_rows, decays, norm_gain[None])


def per_device(inputs, query_weight, key_weight, value_weight, lambda_weight, log_decay, norm_gain):
    qk, lambdas, value_rows = project(
        inputs[0], query_weight, key_weight, value_weight, lambda_weight)
    levels = lambda_weight.shape[1] // log_decay.shape[2]
    return mix_all(qk, lambdas, value_rows, log_decay[0], norm_gain, levels)[None]


def solution(mesh):
    return jax.shard_map(
        per_device,
        mesh=mesh,
        in_specs=(
            P("dp", "ctx", None),
            P("dp", None),
            P("dp", None),
            P("dp", None),
            P("dp", None),
            P("dp", "ctx", None),
            P(),
        ),
        out_specs=P("dp", "ctx", None),
        check_vma=False,
    )
```

```python
import functools
import math

import jax
import jax.numpy as jnp
from jax import lax
from jax.experimental import pallas as pl
from jax.experimental.pallas import tpu as pltpu
from jax.sharding import PartitionSpec as P

HIGHEST = lax.Precision.HIGHEST
MESH = pl.DeviceIdType.MESH
VMEM_LIMIT = 63 * 1024 * 1024


CHUNKS = 16
SHARED = 5
PACK = 4


def gather_kernel(x_ref, a_ref, v_ref, qk_ref, lam_ref, val_ref, big_a, big_v, acc_a, acc_v,
                  direct_sem, core_sem, send_sem, relay_sem, z_sem, fwd_sem,
                  own_a, own_v, own_sem):
    depth = a_ref.shape[0]
    rows = depth // CHUNKS
    half = rows // 2
    direct = CHUNKS - SHARED
    dp = lax.axis_index("dp")
    ctx = lax.axis_index("ctx")
    x_at, y_at = dp % 2, dp // 2
    core = ctx % 2
    side = (ctx // 2) % 2
    to_x = {"dp": y_at * 2 + (1 - x_at)}
    to_y = {"dp": (1 - y_at) * 2 + x_at}
    to_core = {"ctx": ctx + 1 - 2 * core}
    to_z = {"ctx": ctx + 2 - 4 * side}
    owners = (dp, y_at * 2 + (1 - x_at), (1 - y_at) * 2 + x_at, (1 - y_at) * 2 + (1 - x_at))

    def place(i):
        at = i + side * (CHUNKS - 1 - 2 * i)
        return pl.ds(pl.multiple_of(at * rows + core * half, half), half)

    pairs = ((a_ref, big_a), (v_ref, big_v))

    def own_copy(way, i):
        target = to_x if way == 0 else to_y
        return [
            pltpu.make_async_remote_copy(
                src_ref=own.at[place(i)], dst_ref=big.at[way, place(i)],
                send_sem=send_sem.at[way, i, k], recv_sem=direct_sem.at[way, i, k],
                device_id=target, device_id_type=MESH)
            for k, (own, big) in enumerate(pairs)]

    def relay_copy(i):
        way = 0 if i % 2 else 1
        target = to_y if i % 2 else to_x
        return [
            pltpu.make_async_remote_copy(
                src_ref=big.at[way, place(i)], dst_ref=big.at[2, place(i)],
                send_sem=relay_sem.at[i, k], recv_sem=direct_sem.at[2, i, k],
                device_id=target, device_id_type=MESH)
            for k, (own, big) in enumerate(pairs)]

    def z_copy(way, i):
        return [
            pltpu.make_async_remote_copy(
                src_ref=big.at[way, place(i)], dst_ref=big.at[way, place(i)],
                send_sem=z_sem.at[way, i, k], recv_sem=direct_sem.at[way, CHUNKS - 1 - i, k],
                device_id=to_z, device_id_type=MESH)
            for k, (own, big) in enumerate(pairs)]

    def core_copy(way, i):
        return [
            pltpu.make_async_remote_copy(
                src_ref=big.at[way, place(i)], dst_ref=big.at[way, place(i)],
                send_sem=fwd_sem.at[way, i, k], recv_sem=core_sem.at[way, i, k],
                device_id=to_core, device_id_type=MESH)
            for k, (own, big) in enumerate(pairs)]

    started = []

    def start(copies):
        for copy in copies:
            copy.start()
            started.append(copy)

    def arrived(way, i):
        for k, (own, big) in enumerate(pairs):
            spot = big.at[way, place(i)]
            pltpu.make_async_copy(spot, spot, direct_sem.at[way, i, k]).wait()

    barrier = pltpu.get_barrier_semaphore()
    for target in (to_x, to_y, to_core, to_z):
        pl.semaphore_signal(barrier, inc=1, device_id=target, device_id_type=MESH)
    pl.semaphore_wait(barrier, 4)

    for i in range(2):
        start(own_copy(0, i))
        start(own_copy(1, i))
    local = [pltpu.make_async_copy(a_ref, own_a, own_sem.at[0]),
             pltpu.make_async_copy(v_ref, own_v, own_sem.at[1])]
    for copy in local:
        copy.start()
    for copy in local:
        copy.wait()

    own_at = pl.ds(pl.multiple_of(owners[0] * depth, depth), depth)
    tile = 512
    wide = acc_v.shape[1]
    acc_a[...] = jnp.dot(x_ref[:, own_at], own_a[...], preferred_element_type=jnp.float32)

    def first(n, carry):
        cols = pl.ds(pl.multiple_of(n * tile, tile), tile)
        acc_v[:, cols] = jnp.dot(
            x_ref[:, own_at], own_v[:, cols], preferred_element_type=jnp.float32)
        return carry

    lax.fori_loop(0, wide // tile, first, 0)

    def multiply(way, pack):
        span = PACK * rows
        at = pack + side * (CHUNKS // PACK - 1 - 2 * pack)
        low = pl.multiple_of(at * span, span)
        for i in range(PACK * pack, PACK * (pack + 1)):
            for k, (own, big) in enumerate(pairs):
                at_i = i + side * (CHUNKS - 1 - 2 * i)
                other = pl.ds(pl.multiple_of(at_i * rows + (1 - core) * half, half), half)
                spot = big.at[way, other]
                pltpu.make_async_copy(spot, spot, core_sem.at[way, i, k]).wait()
        part = x_ref[:, pl.ds(pl.multiple_of(owners[way + 1] * depth + low, span), span)]
        acc_a[...] += jnp.dot(
            part, big_a[way, pl.ds(low, span)], preferred_element_type=jnp.float32)

        def more(n, carry):
            cols = pl.ds(pl.multiple_of(n * tile, tile), tile)
            acc_v[:, cols] += jnp.dot(
                part, big_v[way, pl.ds(low, span), cols], preferred_element_type=jnp.float32)
            return carry

        lax.fori_loop(0, wide // tile, more, 0)

    ready = []

    def take(way, i):
        arrived(way, i)
        if i < SHARED:
            start(z_copy(way, i))
        if way < 2 and i < direct and way == (0 if i % 2 else 1):
            start(relay_copy(i))
        start(core_copy(way, i))

    seen = {}

    def note(way, i):
        take(way, i)
        pack = (way, i // PACK)
        seen[pack] = seen.get(pack, 0) + 1
        if seen[pack] == PACK:
            ready.append(pack)

    lag = 2
    crossed = []
    for step in range(SHARED + lag):
        crossed += [(way, step) for way in range(2) if step < SHARED]
        crossed += [(2, step - lag)] if step >= lag else []
    taken = 0
    for step in range(direct + lag):
        due, ready[:] = list(ready), []
        if step < direct:
            note(0, step)
            note(1, step)
            if step + 2 < direct:
                start(own_copy(0, step + 2))
                start(own_copy(1, step + 2))
        if step >= lag:
            note(2, step - lag)
        while taken < min(len(crossed), (3 * step - 1) // 2):
            way, i = crossed[taken]
            note(way, CHUNKS - 1 - i)
            taken += 1
        for pack in due:
            multiply(*pack)
    while taken < len(crossed):
        way, i = crossed[taken]
        note(way, CHUNKS - 1 - i)
        taken += 1
    while ready:
        multiply(*ready.pop(0))
    for copy in started:
        copy.wait_send()
    narrow = qk_ref.shape[1]
    qk_ref[...] = acc_a[:, :narrow].astype(jnp.bfloat16)
    lam_ref[...] = jax.nn.softplus(acc_a[:, narrow:])
    val_ref[...] = acc_v[...].astype(jnp.bfloat16)


def project(tokens, query_weight, key_weight, value_weight, lambda_weight):
    length = tokens.shape[0]
    depth, wide = value_weight.shape
    narrow = query_weight.shape[1] + key_weight.shape[1]
    lams = lambda_weight.shape[1]
    fill = -lams % 128
    packed = jnp.concatenate(
        (query_weight, key_weight, lambda_weight, jnp.zeros((depth, fill), jnp.bfloat16)), axis=1)
    columns = packed.shape[1]
    vmem = pl.BlockSpec(memory_space=pltpu.VMEM)
    dma = pltpu.SemaphoreType.DMA
    return pl.pallas_call(
        gather_kernel,
        out_shape=(
            jax.ShapeDtypeStruct((length, narrow), jnp.bfloat16),
            jax.ShapeDtypeStruct((length, lams + fill), jnp.float32),
            jax.ShapeDtypeStruct((length, wide), jnp.bfloat16),
        ),
        in_specs=[vmem] + [pl.BlockSpec(memory_space=pl.ANY)] * 2,
        out_specs=(vmem,) * 3,
        scratch_shapes=[
            pltpu.VMEM((3, depth, columns), jnp.bfloat16),
            pltpu.VMEM((3, depth, wide), jnp.bfloat16),
            pltpu.VMEM((length, columns), jnp.float32),
            pltpu.VMEM((length, wide), jnp.float32),
            dma((3, CHUNKS, 2)),
            dma((3, CHUNKS, 2)),
            dma((2, CHUNKS, 2)),
            dma((CHUNKS, 2)),
            dma((3, SHARED, 2)),
            dma((3, CHUNKS, 2)),
            pltpu.VMEM((depth, columns), jnp.bfloat16),
            pltpu.VMEM((depth, wide), jnp.bfloat16),
            dma((2,)),
        ],
        compiler_params=pltpu.CompilerParams(
            collective_id=0, has_side_effects=True, vmem_limit_bytes=VMEM_LIMIT),
        name="gather_project",
    )(tokens, packed, value_weight)


def flipped(index, mask):
    out = index
    for power in range(mask.bit_length()):
        if mask >> power & 1:
            step = 1 << power
            out = out + step - 2 * step * ((index // step) % 2)
    return out


def mixer_kernel(levels, qk_ref, lam_ref, val_ref, decay_ref, gain_ref, out_ref, logs, state,
                 sent, got, mixed, score, cum, grow, log_send, log_recv, first_send, first_recv,
                 part_send, part_recv, share_send, share_recv):
    count = lax.axis_size("ctx")
    bits = count.bit_length() - 1
    ctx = lax.axis_index("ctx")
    length, heads = decay_ref.shape
    head_dim = val_ref.shape[1] // heads
    state_dim = qk_ref.shape[1] // 2
    inner = length.bit_length()
    scale = 1.0 / math.sqrt(state_dim)
    tile = 128
    tiles = length // tile
    peers = [None] + [{"ctx": flipped(ctx, r)} for r in range(1, count)]
    started = []

    def send(src, dst, out_sem, in_sem, peer):
        copy = pltpu.make_async_remote_copy(
            src_ref=src, dst_ref=dst, send_sem=out_sem, recv_sem=in_sem,
            device_id=peers[peer], device_id_type=MESH)
        copy.start()
        started.append(copy)

    def await_at(spot, sem):
        pltpu.make_async_copy(spot, spot, sem).wait()

    barrier = pltpu.get_barrier_semaphore()
    for r in range(1, count):
        pl.semaphore_signal(barrier, inc=1, device_id=peers[r], device_id_type=MESH)

    row = lax.broadcasted_iota(jnp.int32, (length, length), 0)
    col = lax.broadcasted_iota(jnp.int32, (length, length), 1)
    below = (row >= col).astype(jnp.float32)
    decays = decay_ref[...]
    ones = jnp.ones((length, tile), jnp.float32)
    logs[0] = lax.dot_general(
        decays, ones, (((0,), (0,)), ((), ())), precision=HIGHEST,
        preferred_element_type=jnp.float32)
    cum_col = jnp.dot(below, decays, precision=HIGHEST, preferred_element_type=jnp.float32)
    cum_row = lax.dot_general(
        decays, below, (((0,), (1,)), ((), ())), precision=HIGHEST,
        preferred_element_type=jnp.float32)
    cum[...] = cum_row
    grow[...] = jnp.exp(cum_col) * scale
    remain = jnp.exp(cum_col[length - 1:length] - cum_col)
    pl.semaphore_wait(barrier, count - 1)
    for r in range(1, count):
        send(logs.at[0], logs.at[r], log_send.at[r], log_recv.at[r], r)

    def values_of(h):
        return val_ref[:, h * head_dim:(h + 1) * head_dim]

    keys = qk_ref[:, state_dim:].astype(jnp.float32)
    halves = 2
    for part in range(halves):
        span = heads // halves
        for h in range(part * span, (part + 1) * span):
            keyed = (keys * remain[:, h:h + 1]).astype(jnp.bfloat16)
            block = lax.dot_general(
                keyed, values_of(h), (((0,), (0,)), ((), ())),
                preferred_element_type=jnp.float32)
            state[h] = block
            sent[0, h] = block.astype(jnp.bfloat16)
        if bits > 0:
            at = pl.ds(part * span, span)
            send(sent.at[0, at], got.at[0, at], first_send.at[part], first_recv.at[part], 1)

    trow = lax.broadcasted_iota(jnp.int32, (tile, tile), 0)
    tcol = lax.broadcasted_iota(jnp.int32, (tile, tile), 1)
    differ = jnp.bitwise_xor(trow, tcol)
    depth = tile.bit_length() - 1
    full = lax.dot_general(
        qk_ref[:, :state_dim], qk_ref[:, state_dim:], (((1,), (1,)), ((), ())),
        preferred_element_type=jnp.float32)
    score[...] = jnp.where(row >= col, full * scale, 0.0)

    def near(h):
        base = h * levels
        for ti in range(tiles):
            rows = slice(ti * tile, (ti + 1) * tile)
            total = None
            for tj in range(ti + 1):
                cols = slice(tj * tile, (tj + 1) * tile)
                if ti == tj:
                    weight = jnp.broadcast_to(lam_ref[rows, base:base + 1], (tile, tile))
                    for level in range(1, depth + 1):
                        at = base + level
                        weight = jnp.where(
                            differ >= 1 << (level - 1), lam_ref[rows, at:at + 1], weight)
                else:
                    at = base + depth + (ti ^ tj).bit_length()
                    weight = lam_ref[rows, at:at + 1]
                distance = cum_col[rows, h:h + 1] - cum[h:h + 1, cols]
                decay = jnp.exp(jnp.minimum(distance, 0.0))
                mix = (weight * (decay * score[rows, cols])).astype(jnp.bfloat16)
                term = jnp.dot(
                    mix, val_ref[cols, h * head_dim:(h + 1) * head_dim],
                    preferred_element_type=jnp.float32)
                total = term if total is None else total + term
            mixed[rows, h * head_dim:(h + 1) * head_dim] = total

    left = list(range(heads))

    def near_some(most):
        for _ in range(min(most, len(left))):
            near(left.pop(0))

    def far(b, h, carry, upper):
        carried = (carry[h:h + 1] * got[b, h].astype(jnp.float32)).astype(jnp.bfloat16)
        reach = jnp.dot(qk_ref[:, :state_dim], carried, preferred_element_type=jnp.float32)
        at = h * levels + inner + b
        factor = lam_ref[:, at:at + 1] * grow[:, h:h + 1] * upper
        return factor * reach

    near_some(3)
    for r in range(1, count):
        await_at(logs.at[r], log_recv.at[r])
    own_log = logs[0]
    carry_log = jnp.zeros_like(own_log)
    pending = []
    for b in range(bits):
        upper = ((ctx // (1 << b)) % 2).astype(jnp.float32)
        other_log = logs[1 << b]
        for r in range((1 << b) + 1, 2 << b):
            other_log = other_log + logs[r]
        group = min(1 << b, 4)
        if b == 0:
            for part in range(halves):
                at = pl.ds(part * (heads // halves), heads // halves)
                await_at(got.at[0, at], first_recv.at[part])
        else:
            span = heads // group

            def slot(ref, r):
                return ref.at[b, pl.ds(flipped(ctx % group, r) * span, span)]

            await_at(slot(got, 0), part_recv.at[b])
            for r in range(1, group):
                send(slot(got, 0), slot(got, 0), share_send.at[b, r], share_recv.at[b, r], r)
            near_some(2)
            if b + 1 == bits:
                near_some(heads)
                for p in pending:
                    for h in range(heads):
                        cols = slice(h * head_dim, (h + 1) * head_dim)
                        mixed[:, cols] += far(p[0], h, p[1], p[2])
            for r in range(1, group):
                await_at(slot(got, r), share_recv.at[b, r])
        pending.append((b, jnp.exp(carry_log), upper))
        if b + 1 < bits:
            keep = jnp.where(upper > 0, 1.0, jnp.exp(other_log))
            take = jnp.where(upper > 0, jnp.exp(own_log), 1.0)
            for h in range(heads):
                block = keep[h:h + 1] * state[h] + take[h:h + 1] * got[b, h].astype(jnp.float32)
                state[h] = block
                sent[b + 1, h] = block.astype(jnp.bfloat16)
            ahead = min(2 << b, 4)
            wide = heads // ahead
            at = pl.ds((ctx % ahead) * wide, wide)
            send(sent.at[b + 1, at], got.at[b + 1, at], part_send.at[b + 1],
                 part_recv.at[b + 1], 2 << b)
            carry_log = carry_log + upper * other_log
            own_log = own_log + other_log
            near_some(5)
    near_some(heads)
    rest = pending[-1:] if bits > 1 else pending
    for h in range(heads):
        cols = slice(h * head_dim, (h + 1) * head_dim)
        whole = mixed[:, cols]
        for p in rest:
            whole = whole + far(p[0], h, p[1], p[2])
        mean_square = jnp.mean(whole * whole, axis=-1, keepdims=True)
        out_ref[:, cols] = (whole * lax.rsqrt(mean_square + 1e-05) * gain_ref[:, cols]).astype(
            jnp.bfloat16)
    for copy in started:
        copy.wait_send()


def mix_all(qk, lambdas, value_rows, decays, norm_gain, levels):
    length, heads = decays.shape
    wide = value_rows.shape[1]
    state_dim = qk.shape[1] // 2
    head_dim = wide // heads
    count = lax.axis_size("ctx")
    bits = count.bit_length() - 1
    vmem = pl.BlockSpec(memory_space=pltpu.VMEM)
    dma = pltpu.SemaphoreType.DMA
    return pl.pallas_call(
        functools.partial(mixer_kernel, levels),
        out_shape=jax.ShapeDtypeStruct((length, wide), jnp.bfloat16),
        in_specs=[vmem] * 5,
        out_specs=vmem,
        scratch_shapes=[
            pltpu.VMEM((count, heads, 128), jnp.float32),
            pltpu.VMEM((heads, state_dim, head_dim), jnp.float32),
            pltpu.VMEM((bits, heads, state_dim, head_dim), jnp.bfloat16),
            pltpu.VMEM((bits, heads, state_dim, head_dim), jnp.bfloat16),
            pltpu.VMEM((length, wide), jnp.float32),
            pltpu.VMEM((length, length), jnp.float32),
            pltpu.VMEM((heads, length), jnp.float32),
            pltpu.VMEM((length, heads), jnp.float32),
            dma((count,)),
            dma((count,)),
            dma((2,)),
            dma((2,)),
            dma((bits,)),
            dma((bits,)),
            dma((bits, 4)),
            dma((bits, 4)),
        ],
        compiler_params=pltpu.CompilerParams(
            collective_id=1, has_side_effects=True, vmem_limit_bytes=VMEM_LIMIT),
        name="mixer",
    )(qk, lambdas, value_rows, decays, norm_gain[None])


def per_device(inputs, query_weight, key_weight, value_weight, lambda_weight, log_decay, norm_gain):
    qk, lambdas, value_rows = project(
        inputs[0], query_weight, key_weight, value_weight, lambda_weight)
    levels = lambda_weight.shape[1] // log_decay.shape[2]
    return mix_all(qk, lambdas, value_rows, log_decay[0], norm_gain, levels)[None]


def solution(mesh):
    return jax.shard_map(
        per_device,
        mesh=mesh,
        in_specs=(
            P("dp", "ctx", None),
            P("dp", None),
            P("dp", None),
            P("dp", None),
            P("dp", None),
            P("dp", "ctx", None),
            P(),
        ),
        out_specs=P("dp", "ctx", None),
        check_vma=False,
    )
```
